32 devices in a mesh: blk: 16 (over z, y, core), uly: 2 (over x).
Axes of the slice: x: 2, y: 2, z: 4, core: 2. Of those that a mesh axis runs over, the one named last changes fastest.
Arguments:
- tokens: bfloat16 [4096, 5120], P(('blk', 'uly')), may hold values from -6 to 6
- query_base: bfloat16 [4096, 5120], P(('blk', 'uly')), may hold values from -9 to 9
- key_base: bfloat16 [4096, 5120], P(('blk', 'uly')), may hold values from -9 to 9
- value_base: bfloat16 [4096, 5120], P(('blk', 'uly')), may hold values from -6 to 6
- out_grad: bfloat16 [4096, 5120], P(('blk', 'uly')), may hold values from -0.059814453 to 0.059814453
- down_q: bfloat16 [5120, 64], replicated, may hold values from -0.078125 to 0.078125
- up_q: bfloat16 [64, 5120], replicated, may hold values from -0.75 to 0.75
- down_v: bfloat16 [5120, 64], replicated, may hold values from -0.078125 to 0.078125
- up_v: bfloat16 [64, 5120], replicated, may hold values from -0.75 to 0.75
Outputs:
- attended: bfloat16 [4096, 5120], P(('blk', 'uly'))
- grad_down_q: bfloat16 [5120, 64], replicated
- grad_up_q: bfloat16 [64, 5120], P(None, 'uly')
- grad_down_v: bfloat16 [5120, 64], replicated
- grad_up_v: bfloat16 [64, 5120], P(None, 'uly')
The draws below stay inside these ranges and needn't reach their ends.
All inputs are finite; a program needn't handle non-finite values.
Results may differ from the reference program's by a relative error of at most 0.025.
Values may be sent and summed in bfloat16 or wider, within the bound.
A program may use at most 128 MiB of HBM per device.

```python
import jax
import jax.numpy as jnp
from jax import lax

D = 5120
HEADS = 40
HEAD = 128
RANK = 64
BLOCK = 256
TOKENS = 4096


def shared_bases(key):
    base = jax.random.fold_in(key, 7)
    key_query, key_keys = jax.random.split(base, 2)
    query = jnp.clip(1.5 * jax.random.normal(key_query, (TOKENS, D), jnp.float32), -9.0, 9.0)
    keys = jnp.clip(1.5 * jax.random.normal(key_keys, (TOKENS, D), jnp.float32), -9.0, 9.0)
    return (query, keys)


def draw_query_base(key, part):
    return shared_bases(key)[0].astype(jnp.bfloat16)


def draw_key_base(key, part):
    return shared_bases(key)[1].astype(jnp.bfloat16)


def shard_levels(rng, dims, shards, low, top_value):
    gain = 1.0
    for axis_at, blocks in shards:
        steps = jax.random.uniform(jax.random.fold_in(jax.random.fold_in(rng, 6), axis_at), (blocks,), jnp.float32, low / len(shards), top_value / len(shards))
        gain = gain * jnp.repeat(jnp.exp(steps), dims[axis_at] // blocks).reshape((-1,) + (1,) * (len(dims) - 1 - axis_at))
    return gain


def scatter_about(own_key, dims, deviation, bound, cuts=(), held_as=jnp.bfloat16):
    result = jax.random.normal(own_key, dims, jnp.float32) * deviation
    if len(cuts) > 0:
        result = shard_levels(own_key, dims, cuts, -0.22, 0.18) * result
    return jnp.clip(result, min=-bound, max=bound).astype(held_as)


def setup_inputs(seed: int = 0) -> dict:
    key_of = jax.random.split(jax.random.key(seed), 10)
    tokens = scatter_about(key_of[0], (TOKENS, D), 1.0, 6.0, ((0, 32),))
    query_base = draw_query_base(jax.random.fold_in(key_of[9], 71), 0)
    key_base = draw_key_base(jax.random.fold_in(key_of[9], 71), 0)
    value_base = scatter_about(key_of[3], (TOKENS, D), 1.0, 6.0, ((0, 32),))
    out_grad = scatter_about(key_of[4], (TOKENS, D), 0.01, 0.059814453, ((0, 32),))
    down_q = scatter_about(key_of[5], (D, RANK), D ** -0.5, 0.078125)
    up_q = scatter_about(key_of[6], (RANK, D), RANK ** -0.5, 0.75)
    down_v = scatter_about(key_of[7], (D, RANK), D ** -0.5, 0.078125)
    up_v = scatter_about(key_of[8], (RANK, D), RANK ** -0.5, 0.75)
    return {"tokens": tokens, "query_base": query_base, "key_base": key_base, "value_base": value_base, "out_grad": out_grad, "down_q": down_q, "up_q": up_q, "down_v": down_v, "up_v": up_v}


def inner(left, right):
    return lax.dot_general(left, right, (((0,), (0,)), ((), ())), preferred_element_type=jnp.float32)


def head_pass(query, keys, values, upstream, usable, scale):
    scores = jnp.dot(query, keys.T, preferred_element_type=jnp.float32) * scale
    scores = jnp.where(usable[None, :], scores, -jnp.inf)
    top = jnp.max(scores, axis=1, keepdims=True)
    total = jnp.sum(jnp.exp(scores - top), axis=1, keepdims=True)
    probs = jnp.exp(scores - top - jnp.log(total)).astype(jnp.bfloat16)
    attended = jnp.dot(probs, values, preferred_element_type=jnp.float32).astype(jnp.bfloat16)
    delta = jnp.sum(upstream.astype(jnp.float32) * attended.astype(jnp.float32), axis=1, keepdims=True)
    prob_grad = jnp.dot(upstream, values.T, preferred_element_type=jnp.float32)
    score_grad = (probs.astype(jnp.float32) * (prob_grad - delta)).astype(jnp.bfloat16)
    query_grad = (jnp.dot(score_grad, keys, preferred_element_type=jnp.float32) * scale).astype(jnp.bfloat16)
    value_terms = jnp.dot(probs.T, upstream, preferred_element_type=jnp.float32)
    return attended, query_grad, value_terms


def reference(tokens, query_base, key_base, value_base, out_grad, down_q, up_q, down_v, up_v):
    low_q = jnp.dot(tokens, down_q, preferred_element_type=jnp.float32).astype(jnp.bfloat16)
    low_v = jnp.dot(tokens, down_v, preferred_element_type=jnp.float32).astype(jnp.bfloat16)
    query = (query_base.astype(jnp.float32) + jnp.dot(low_q, up_q, preferred_element_type=jnp.float32)).astype(jnp.bfloat16)
    value = (value_base.astype(jnp.float32) + jnp.dot(low_v, up_v, preferred_element_type=jnp.float32)).astype(jnp.bfloat16)
    nblocks = TOKENS // BLOCK

    def blocks(array):
        return array.reshape(nblocks, BLOCK, HEADS, HEAD).transpose(0, 2, 1, 3)

    query_b = blocks(query)
    keys_b = blocks(key_base)
    values_b = blocks(value)
    upstream_b = blocks(out_grad)
    keys_p = jnp.concatenate([jnp.zeros_like(keys_b[:1]), keys_b[:-1]], 0)
    values_p = jnp.concatenate([jnp.zeros_like(values_b[:1]), values_b[:-1]], 0)
    column = jnp.arange(2 * BLOCK)
    scale = HEAD ** -0.5
    first = jnp.arange(nblocks) == 0

    def per_block(items):
        q_blk, k_blk, kp_blk, v_blk, vp_blk, g_blk, leading = items
        usable = jnp.logical_or(column >= BLOCK, jnp.logical_not(leading))

        def per_head(parts):
            q_one, k_one, kp_one, v_one, vp_one, g_one = parts
            return head_pass(q_one, jnp.concatenate([kp_one, k_one], 0), jnp.concatenate([vp_one, v_one], 0), g_one, usable, scale)

        return lax.map(per_head, (q_blk, k_blk, kp_blk, v_blk, vp_blk, g_blk))

    attended_b, query_grad_b, value_terms = lax.map(per_block, (query_b, keys_b, keys_p, values_b, values_p, upstream_b, first))
    prior_part = value_terms[:, :, :BLOCK]
    own_part = value_terms[:, :, BLOCK:]
    incoming = jnp.concatenate([prior_part[1:], jnp.zeros_like(prior_part[:1])], 0)
    value_grad_b = (own_part + incoming).astype(jnp.bfloat16)

    def unblock(array):
        return array.transpose(0, 2, 1, 3).reshape(TOKENS, D)

    attended = unblock(attended_b)
    query_grad = unblock(query_grad_b)
    value_grad = unblock(value_grad_b)
    lowrank = jnp.concatenate([
        jnp.dot(query_grad, up_q.T, preferred_element_type=jnp.float32),
        jnp.dot(value_grad, up_v.T, preferred_element_type=jnp.float32)], 1).astype(jnp.bfloat16)
    down_total = inner(tokens, lowrank)
    grad_down_q = down_total[:, :RANK].astype(jnp.bfloat16)
    grad_down_v = down_total[:, RANK:].astype(jnp.bfloat16)
    grad_up_q = inner(low_q, query_grad).astype(jnp.bfloat16)
    grad_up_v = inner(low_v, value_grad).astype(jnp.bfloat16)
    return attended, grad_down_q, grad_up_q, grad_down_v, grad_up_v
```

```python
import functools

import jax
import jax.numpy as jnp
from jax import lax
from jax.experimental import pallas as pl
from jax.experimental.pallas import tpu as pltpu
from jax.sharding import PartitionSpec as P

HEAD = 128
CHUNK = 512
MESH = pl.DeviceIdType.MESH
F32 = jnp.float32
BF16 = jnp.bfloat16


def inner(left, right):
    return lax.dot_general(left, right, (((0,), (0,)), ((), ())), preferred_element_type=F32)


def outer(left, right):
    return lax.dot_general(left, right, (((1,), (1,)), ((), ())), preferred_element_type=F32)


def dot(left, right):
    return jnp.dot(left, right, preferred_element_type=F32)


def attention_kernel(
    nb, nu,
    tokens, query_base, key_base, value_base, out_grad, down_q, up_q, down_v, up_v,
    att_ref, gup_ref, low_out,
    kbuf, vbuf, lbuf, tok, qs, gs, dq, dv, ups, lrq, lrv, lrin,
    local_sem, xsend, xrecv, fsend, frecv, lsend, lrecv, msend, mrecv, rsend, rrecv,
):
    blk = lax.axis_index("blk")
    u = lax.axis_index("uly")
    rows, width = tokens.shape
    rank = up_q.shape[0]
    span = nu * rows
    chunks = width // CHUNK
    has_prev = blk > 0
    has_next = blk < nb - 1
    mine = pl.ds(pl.multiple_of(span + u * rows, rows), rows)

    def peer(j):
        return lax.rem(u + j, nu)

    def source(j):
        return lax.rem(u - j + nu, nu)

    def cols(c):
        return pl.ds(pl.multiple_of(c * CHUNK, CHUNK), CHUNK)

    barrier = pltpu.get_barrier_semaphore()
    for j in range(1, nu):
        pl.semaphore_signal(barrier, inc=1, device_id=(blk, peer(j)), device_id_type=MESH)

    @pl.when(has_prev)
    def _():
        for j in range(nu):
            pl.semaphore_signal(barrier, inc=1, device_id=(blk - 1, peer(j)), device_id_type=MESH)

    @pl.when(has_next)
    def _():
        for j in range(nu):
            pl.semaphore_signal(barrier, inc=1, device_id=(blk + 1, peer(j)), device_id_type=MESH)

    local = [
        pltpu.make_async_copy(src, dst, local_sem.at[i])
        for i, (src, dst) in enumerate(
            (
                (tokens, tok), (down_v, dv), (down_q, dq),
                (up_q, ups.at[pl.ds(0, rank)]), (up_v, ups.at[pl.ds(rank, rank)]),
                (value_base, vbuf.at[mine]), (key_base, kbuf.at[mine]),
                (query_base, qs), (out_grad, gs),
            )
        )
    ]
    for copy in local:
        copy.start()

    edge = jnp.logical_or(blk == 0, blk == nb - 1)

    @pl.when(edge)
    def _():
        pl.semaphore_wait(barrier, 2 * nu - 1)

    @pl.when(jnp.logical_not(edge))
    def _():
        pl.semaphore_wait(barrier, 3 * nu - 1)

    bufs = (kbuf, vbuf)

    def across(a, j, c):
        src = key_base.at[:, cols(c)] if a == 0 else vbuf.at[mine, cols(c)]
        return pltpu.make_async_remote_copy(
            src_ref=src, dst_ref=bufs[a].at[mine, cols(c)],
            send_sem=xsend.at[a, j, c], recv_sem=xrecv.at[a, j, c],
            device_id=(blk, peer(j)), device_id_type=MESH,
        )

    def crossed(a, j, c):
        here = bufs[a].at[pl.ds(pl.multiple_of(span + source(j) * rows, rows), rows), cols(c)]
        return pltpu.make_async_remote_copy(
            src_ref=here, dst_ref=here,
            send_sem=xsend.at[a, j, c], recv_sem=xrecv.at[a, j, c],
            device_id=(blk, peer(j)), device_id_type=MESH,
        )

    def onward(a, j, c):
        s = source(j)
        if a == 0 and j == 0:
            src = key_base.at[:, cols(c)]
        else:
            src = bufs[a].at[pl.ds(pl.multiple_of(span + s * rows, rows), rows), cols(c)]
        return pltpu.make_async_remote_copy(
            src_ref=src, dst_ref=bufs[a].at[pl.ds(pl.multiple_of(s * rows, rows), rows), cols(c)],
            send_sem=fsend.at[a, j, c], recv_sem=frecv.at[a, j, c],
            device_id=(blk + 1, u), device_id_type=MESH,
        )

    def arrived(a, j, c):
        here = bufs[a].at[pl.ds(pl.multiple_of(source(j) * rows, rows), rows), cols(c)]
        return pltpu.make_async_remote_copy(
            src_ref=here, dst_ref=here,
            send_sem=fsend.at[a, j, c], recv_sem=frecv.at[a, j, c],
            device_id=(blk, peer(1)), device_id_type=MESH,
        )

    def low_across(j):
        return pltpu.make_async_remote_copy(
            src_ref=lbuf.at[mine], dst_ref=lbuf.at[mine],
            send_sem=lsend.at[j], recv_sem=lrecv.at[j],
            device_id=(blk, peer(j)), device_id_type=MESH,
        )

    def low_crossed(j):
        here = lbuf.at[pl.ds(pl.multiple_of(span + source(j) * rows, rows), rows)]
        return pltpu.make_async_remote_copy(
            src_ref=here, dst_ref=here, send_sem=lsend.at[j], recv_sem=lrecv.at[j],
            device_id=(blk, peer(j)), device_id_type=MESH,
        )

    def low_onward(j):
        s = source(j)
        return pltpu.make_async_remote_copy(
            src_ref=lbuf.at[pl.ds(pl.multiple_of(span + s * rows, rows), rows)],
            dst_ref=lbuf.at[pl.ds(pl.multiple_of(s * rows, rows), rows)],
            send_sem=msend.at[j], recv_sem=mrecv.at[j],
            device_id=(blk + 1, u), device_id_type=MESH,
        )

    def low_arrived(j):
        here = lbuf.at[pl.ds(pl.multiple_of(source(j) * rows, rows), rows)]
        return pltpu.make_async_remote_copy(
            src_ref=here, dst_ref=here, send_sem=msend.at[j], recv_sem=mrecv.at[j],
            device_id=(blk, peer(1)), device_id_type=MESH,
        )

    early = min(3, chunks)
    for c in range(early):
        for j in range(1, nu):
            across(0, j, c).start()

        @pl.when(has_next)
        def _():
            onward(0, 0, c).start()

    lane = lax.broadcasted_iota(jnp.int32, (rows, 2 * rank), 1)
    for i in range(3):
        local[i].wait()
    low = jnp.concatenate([dot(tok[...], dq[...]), dot(tok[...], dv[...])], axis=1)
    low_qm = jnp.where(lane < rank, low, 0.0).astype(BF16)
    low_vm = jnp.where(lane >= rank, low, 0.0).astype(BF16)
    lbuf[mine, :] = low_vm
    for i in range(3, 6):
        local[i].wait()

    @pl.loop(0, chunks)
    def _(c):
        part = dot(low_vm, ups[:, cols(c)])
        vbuf[mine, cols(c)] = (vbuf[mine, cols(c)].astype(F32) + part).astype(BF16)

    for j in range(1, nu):
        low_across(j).start()

    @pl.when(has_next)
    def _():
        low_onward(0).start()

    @pl.loop(0, chunks)
    def _(c):
        @pl.when(c >= early)
        def _():
            for j in range(1, nu):
                across(0, j, c).start()

            @pl.when(has_next)
            def _():
                onward(0, 0, c).start()

        for j in range(1, nu):
            across(1, j, c).start()

        @pl.when(has_next)
        def _():
            onward(1, 0, c).start()

    lrq[...] = jnp.zeros_like(lrq)
    lrv[...] = jnp.zeros_like(lrv)

    @pl.when(jnp.logical_not(has_prev))
    def _():
        kbuf[pl.ds(0, span), :] = jnp.zeros((span, width), BF16)
        vbuf[pl.ds(0, span), :] = jnp.zeros((span, width), BF16)
        lbuf[pl.ds(0, span), :] = jnp.zeros((span, 2 * rank), BF16)

    for i in range(6, 9):
        local[i].wait()

    scale = HEAD ** (-0.5)
    key_at = lax.broadcasted_iota(jnp.int32, (rows, 2 * span), 1)
    usable = jnp.logical_or(key_at >= span, has_prev)

    def head(h):
        at = pl.ds(pl.multiple_of(h * HEAD, HEAD), HEAD)
        up = ups[:, at]
        keys = kbuf[:, at]
        values = vbuf[:, at]
        grad = gs[:, at]
        query = (qs[:, at].astype(F32) + dot(low_qm, up)).astype(BF16)
        scores = jnp.where(usable, outer(query, keys) * scale, -jnp.inf)
        weights = jnp.exp(scores - jnp.max(scores, axis=1, keepdims=True))
        total = jnp.sum(weights, axis=1, keepdims=True)
        probs = (weights * (1.0 / total)).astype(BF16)
        attended = dot(probs, values).astype(BF16)
        att_ref[:, at] = attended
        delta = jnp.sum(grad.astype(F32) * attended.astype(F32), axis=1, keepdims=True)
        score_grad = (probs.astype(F32) * (outer(grad, values) - delta)).astype(BF16)
        query_grad = (dot(score_grad, keys) * scale).astype(BF16)
        seen = dot(probs, lbuf[...]).astype(BF16)
        gup_ref[:, at] = (inner(low_qm, query_grad) + inner(seen, grad)).astype(BF16)
        lrq[...] += jnp.where(lane < rank, outer(query_grad, up), 0.0)
        lifted = jnp.where(lane >= rank, outer(grad, up), 0.0).astype(BF16)
        lrv[...] += inner(probs, lifted)

    heads = CHUNK // HEAD

    @pl.loop(0, chunks + 1)
    def _(c):
        @pl.when(c == 0)
        def _():
            for j in range(1, nu):
                low_crossed(j).wait_recv()

                @pl.when(has_next)
                def _():
                    low_onward(j).start()

            @pl.when(has_prev)
            def _():
                for j in range(nu):
                    low_arrived(j).wait_recv()

        @pl.when(c < chunks)
        def _():
            for a in range(2):
                for j in range(1, nu):
                    crossed(a, j, c).wait_recv()

                    @pl.when(has_next)
                    def _():
                        onward(a, j, c).start()

        @pl.when(c > 0)
        def _():
            @pl.when(has_prev)
            def _():
                for a in range(2):
                    for j in range(nu):
                        arrived(a, j, c - 1).wait_recv()

            @pl.loop(0, heads)
            def _(i):
                head((c - 1) * heads + i)

    def terms(k, j, base):
        s = peer(j)
        return pltpu.make_async_remote_copy(
            src_ref=lrv.at[pl.ds(pl.multiple_of(base + s * rows, rows), rows)],
            dst_ref=lrin.at[k, j],
            send_sem=rsend.at[k, j], recv_sem=rrecv.at[k, j],
            device_id=(blk - k, s), device_id_type=MESH,
        )

    for j in range(1, nu):
        terms(0, j, span).start()

    @pl.when(has_prev)
    def _():
        for j in range(nu):
            terms(1, j, 0).start()

    @pl.loop(0, chunks)
    def _(c):
        for a in range(2):
            for j in range(1, nu):
                across(a, j, c).wait_send()

            @pl.when(has_next)
            def _():
                for j in range(nu):
                    onward(a, j, c).wait_send()

    for j in range(1, nu):
        low_across(j).wait_send()

    @pl.when(has_next)
    def _():
        for j in range(nu):
            low_onward(j).wait_send()

    lrq[...] += lrv[mine, :]
    for j in range(1, nu):
        terms(0, j, span).wait_recv()
        lrq[...] += lrin[0, j]

    @pl.when(has_next)
    def _():
        for j in range(nu):
            terms(1, j, 0).wait_recv()
            lrq[...] += lrin[1, j]

    low_out[...] = lrq[...].astype(BF16)
    for j in range(1, nu):
        terms(0, j, span).wait_send()

    @pl.when(has_prev)
    def _():
        for j in range(nu):
            terms(1, j, 0).wait_send()


def attention(nb, nu, *operands):
    rows, width = operands[0].shape
    rank = operands[6].shape[0]
    span = nu * rows
    chunks = width // CHUNK
    dma = pltpu.SemaphoreType.DMA
    anywhere = pl.BlockSpec(memory_space=pl.ANY)
    here = pl.BlockSpec(memory_space=pltpu.VMEM)
    return pl.pallas_call(
        functools.partial(attention_kernel, nb, nu),
        out_shape=(
            jax.ShapeDtypeStruct((rows, width), BF16),
            jax.ShapeDtypeStruct((2 * rank, width), BF16),
            jax.ShapeDtypeStruct((rows, 2 * rank), BF16),
        ),
        in_specs=[anywhere] * 9,
        out_specs=(here, here, here),
        scratch_shapes=[
            pltpu.VMEM((2 * span, width), BF16),
            pltpu.VMEM((2 * span, width), BF16),
            pltpu.VMEM((2 * span, 2 * rank), BF16),
            pltpu.VMEM((rows, width), BF16),
            pltpu.VMEM((rows, width), BF16),
            pltpu.VMEM((rows, width), BF16),
            pltpu.VMEM((width, rank), BF16),
            pltpu.VMEM((width, rank), BF16),
            pltpu.VMEM((2 * rank, width), BF16),
            pltpu.VMEM((rows, 2 * rank), F32),
            pltpu.VMEM((2 * span, 2 * rank), F32),
            pltpu.VMEM((2, nu, rows, 2 * rank), F32),
            dma((9,)),
            dma((2, nu, chunks)), dma((2, nu, chunks)),
            dma((2, nu, chunks)), dma((2, nu, chunks)),
            dma((nu,)), dma((nu,)), dma((nu,)), dma((nu,)),
            dma((2, nu)), dma((2, nu)),
        ],
        compiler_params=pltpu.CompilerParams(
            collective_id=0, has_side_effects=True, vmem_limit_bytes=65_000_000
        ),
    )(*operands)


def per_device(nb, nu, tokens, query_base, key_base, value_base, out_grad, down_q, up_q, down_v, up_v):
    rank = down_q.shape[1]
    attended, gup, lowrank = attention(
        nb, nu, tokens, query_base, key_base, value_base, out_grad, down_q, up_q, down_v, up_v
    )
    down_total = lax.psum(inner(tokens, lowrank).astype(BF16), ("blk", "uly"))
    gup = lax.psum_scatter(gup, "uly", scatter_dimension=1, tiled=True)
    gup = lax.psum(gup, "blk")
    return (
        attended,
        down_total[:, :rank],
        gup[:rank],
        down_total[:, rank:],
        gup[rank:],
    )


def solution(mesh):
    split = P(("blk", "uly"), None)
    return jax.shard_map(
        functools.partial(per_device, mesh.shape["blk"], mesh.shape["uly"]),
        mesh=mesh,
        in_specs=(split,) * 5 + (P(),) * 4,
        out_specs=(split, P(), P(None, "uly"), P(), P(None, "uly")),
        check_vma=False,
    )
```

```python
import functools

import jax
import jax.numpy as jnp
from jax import lax
from jax.experimental import pallas as pl
from jax.experimental.pallas import tpu as pltpu
from jax.sharding import PartitionSpec as P

HEAD = 128
CHUNK = 512
MESH = pl.DeviceIdType.MESH
F32 = jnp.float32
BF16 = jnp.bfloat16


def inner(left, right):
    return lax.dot_general(left, right, (((0,), (0,)), ((), ())), preferred_element_type=F32)


def outer(left, right):
    return lax.dot_general(left, right, (((1,), (1,)), ((), ())), preferred_element_type=F32)


def dot(left, right):
    return jnp.dot(left, right, preferred_element_type=F32)


def attention_kernel(
    nb, nu,
    tokens, query_base, key_base, value_base, out_grad, down_q, up_q, down_v, up_v,
    att_ref, gup_ref, low_out,
    kbuf, vbuf, lbuf, tok, qs, gs, dq, dv, ups, lrq, lrv, lrin,
    local_sem, xsend, xrecv, fsend, frecv, lsend, lrecv, msend, mrecv, rsend, rrecv,
):
    blk = lax.axis_index("blk")
    u = lax.axis_index("uly")
    rows, width = tokens.shape
    rank = up_q.shape[0]
    span = nu * rows
    chunks = width // CHUNK
    has_prev = blk > 0
    has_next = blk < nb - 1
    mine = pl.ds(pl.multiple_of(span + u * rows, rows), rows)

    def peer(j):
        return lax.rem(u + j, nu)

    def source(j):
        return lax.rem(u - j + nu, nu)

    def cols(c):
        return pl.ds(pl.multiple_of(c * CHUNK, CHUNK), CHUNK)

    barrier = pltpu.get_barrier_semaphore()
    for j in range(1, nu):
        pl.semaphore_signal(barrier, inc=1, device_id=(blk, peer(j)), device_id_type=MESH)

    @pl.when(has_prev)
    def _():
        for j in range(nu):
            pl.semaphore_signal(barrier, inc=1, device_id=(blk - 1, peer(j)), device_id_type=MESH)

    @pl.when(has_next)
    def _():
        for j in range(nu):
            pl.semaphore_signal(barrier, inc=1, device_id=(blk + 1, peer(j)), device_id_type=MESH)

    local = [
        pltpu.make_async_copy(src, dst, local_sem.at[i])
        for i, (src, dst) in enumerate(
            (
                (tokens, tok), (down_v, dv), (down_q, dq),
                (up_q, ups.at[pl.ds(0, rank)]), (up_v, ups.at[pl.ds(rank, rank)]),
                (value_base, vbuf.at[mine]), (key_base, kbuf.at[mine]),
                (query_base, qs), (out_grad, gs),
            )
        )
    ]
    for copy in local:
        copy.start()

    edge = jnp.logical_or(blk == 0, blk == nb - 1)

    @pl.when(edge)
    def _():
        pl.semaphore_wait(barrier, 2 * nu - 1)

    @pl.when(jnp.logical_not(edge))
    def _():
        pl.semaphore_wait(barrier, 3 * nu - 1)

    bufs = (kbuf, vbuf)

    def across(a, j, c):
        src = key_base.at[:, cols(c)] if a == 0 else vbuf.at[mine, cols(c)]
        return pltpu.make_async_remote_copy(
            src_ref=src, dst_ref=bufs[a].at[mine, cols(c)],
            send_sem=xsend.at[a, j, c], recv_sem=xrecv.at[a, j, c],
            device_id=(blk, peer(j)), device_id_type=MESH,
        )

    def crossed(a, j, c):
        here = bufs[a].at[pl.ds(pl.multiple_of(span + source(j) * rows, rows), rows), cols(c)]
        return pltpu.make_async_remote_copy(
            src_ref=here, dst_ref=here,
            send_sem=xsend.at[a, j, c], recv_sem=xrecv.at[a, j, c],
            device_id=(blk, peer(j)), device_id_type=MESH,
        )

    def onward(a, j, c):
        s = source(j)
        if a == 0 and j == 0:
            src = key_base.at[:, cols(c)]
        else:
            src = bufs[a].at[pl.ds(pl.multiple_of(span + s * rows, rows), rows), cols(c)]
        return pltpu.make_async_remote_copy(
            src_ref=src, dst_ref=bufs[a].at[pl.ds(pl.multiple_of(s * rows, rows), rows), cols(c)],
            send_sem=fsend.at[a, j, c], recv_sem=frecv.at[a, j, c],
            device_id=(blk + 1, u), device_id_type=MESH,
        )

    def arrived(a, j, c):
        here = bufs[a].at[pl.ds(pl.multiple_of(source(j) * rows, rows), rows), cols(c)]
        return pltpu.make_async_remote_copy(
            src_ref=here, dst_ref=here,
            send_sem=fsend.at[a, j, c], recv_sem=frecv.at[a, j, c],
            device_id=(blk, peer(1)), device_id_type=MESH,
        )

    def low_across(j):
        return pltpu.make_async_remote_copy(
            src_ref=lbuf.at[mine], dst_ref=lbuf.at[mine],
            send_sem=lsend.at[j], recv_sem=lrecv.at[j],
            device_id=(blk, peer(j)), device_id_type=MESH,
        )

    def low_crossed(j):
        here = lbuf.at[pl.ds(pl.multiple_of(span + source(j) * rows, rows), rows)]
        return pltpu.make_async_remote_copy(
            src_ref=here, dst_ref=here, send_sem=lsend.at[j], recv_sem=lrecv.at[j],
            device_id=(blk, peer(j)), device_id_type=MESH,
        )

    def low_onward(j):
        s = source(j)
        return pltpu.make_async_remote_copy(
            src_ref=lbuf.at[pl.ds(pl.multiple_of(span + s * rows, rows), rows)],
            dst_ref=lbuf.at[pl.ds(pl.multiple_of(s * rows, rows), rows)],
            send_sem=msend.at[j], recv_sem=mrecv.at[j],
            device_id=(blk + 1, u), device_id_type=MESH,
        )

    def low_arrived(j):
        here = lbuf.at[pl.ds(pl.multiple_of(source(j) * rows, rows), rows)]
        return pltpu.make_async_remote_copy(
            src_ref=here, dst_ref=here, send_sem=msend.at[j], recv_sem=mrecv.at[j],
            device_id=(blk, peer(1)), device_id_type=MESH,
        )

    early = min(3, chunks)
    for c in range(early):
        for j in range(1, nu):
            across(0, j, c).start()

        @pl.when(has_next)
        def _():
            onward(0, 0, c).start()

    lane = lax.broadcasted_iota(jnp.int32, (rows, 2 * rank), 1)
    for i in range(3):
        local[i].wait()
    low = jnp.concatenate([dot(tok[...], dq[...]), dot(tok[...], dv[...])], axis=1)
    low_qm = jnp.where(lane < rank, low, 0.0).astype(BF16)
    low_vm = jnp.where(lane >= rank, low, 0.0).astype(BF16)
    lbuf[mine, :] = low_vm
    for i in range(3, 6):
        local[i].wait()

    @pl.loop(0, chunks)
    def _(c):
        part = dot(low_vm, ups[:, cols(c)])
        vbuf[mine, cols(c)] = (vbuf[mine, cols(c)].astype(F32) + part).astype(BF16)

    for j in range(1, nu):
        low_across(j).start()

    @pl.when(has_next)
    def _():
        low_onward(0).start()

    @pl.loop(0, chunks)
    def _(c):
        @pl.when(c >= early)
        def _():
            for j in range(1, nu):
                across(0, j, c).start()

            @pl.when(has_next)
            def _():
                onward(0, 0, c).start()

        for j in range(1, nu):
            across(1, j, c).start()

        @pl.when(has_next)
        def _():
            onward(1, 0, c).start()

    lrq[...] = jnp.zeros_like(lrq)
    lrv[...] = jnp.zeros_like(lrv)

    @pl.when(jnp.logical_not(has_prev))
    def _():
        kbuf[pl.ds(0, span), :] = jnp.zeros((span, width), BF16)
        vbuf[pl.ds(0, span), :] = jnp.zeros((span, width), BF16)
        lbuf[pl.ds(0, span), :] = jnp.zeros((span, 2 * rank), BF16)

    for i in range(6, 9):
        local[i].wait()

    scale = HEAD ** (-0.5)
    key_at = lax.broadcasted_iota(jnp.int32, (rows, 2 * span), 1)
    usable = jnp.logical_or(key_at >= span, has_prev)

    def head(h):
        at = pl.ds(pl.multiple_of(h * HEAD, HEAD), HEAD)
        up = ups[:, at]
        keys = kbuf[:, at]
        values = vbuf[:, at]
        grad = gs[:, at]
        query = (qs[:, at].astype(F32) + dot(low_qm, up)).astype(BF16)
        scores = jnp.where(usable, outer(query, keys) * scale, -jnp.inf)
        weights = jnp.exp(scores - jnp.max(scores, axis=1, keepdims=True))
        total = jnp.sum(weights, axis=1, keepdims=True)
        probs = (weights * (1.0 / total)).astype(BF16)
        attended = dot(probs, values).astype(BF16)
        att_ref[:, at] = attended
        delta = jnp.sum(grad.astype(F32) * attended.astype(F32), axis=1, keepdims=True)
        score_grad = (probs.astype(F32) * (outer(grad, values) - delta)).astype(BF16)
        query_grad = (dot(score_grad, keys) * scale).astype(BF16)
        seen = dot(probs, lbuf[...]).astype(BF16)
        here = pl.ds(pl.multiple_of(h * 2 * rank, 2 * rank), 2 * rank)
        gup_ref[here, :] = (inner(low_qm, query_grad) + inner(seen, grad)).astype(BF16)
        lrq[...] += jnp.where(lane < rank, outer(query_grad, up), 0.0)
        lifted = jnp.where(lane >= rank, outer(grad, up), 0.0).astype(BF16)
        lrv[...] += inner(probs, lifted)

    heads = CHUNK // HEAD

    @pl.loop(0, chunks + 1)
    def _(c):
        @pl.when(c == 0)
        def _():
            for j in range(1, nu):
                low_crossed(j).wait_recv()

                @pl.when(has_next)
                def _():
                    low_onward(j).start()

            @pl.when(has_prev)
            def _():
                for j in range(nu):
                    low_arrived(j).wait_recv()

        @pl.when(c < chunks)
        def _():
            for a in range(2):
                for j in range(1, nu):
                    crossed(a, j, c).wait_recv()

                    @pl.when(has_next)
                    def _():
                        onward(a, j, c).start()

        @pl.when(c > 0)
        def _():
            @pl.when(has_prev)
            def _():
                for a in range(2):
                    for j in range(nu):
                        arrived(a, j, c - 1).wait_recv()

            @pl.loop(0, heads)
            def _(i):
                head((c - 1) * heads + i)

    def terms(k, j, base):
        s = peer(j)
        return pltpu.make_async_remote_copy(
            src_ref=lrv.at[pl.ds(pl.multiple_of(base + s * rows, rows), rows)],
            dst_ref=lrin.at[k, j],
            send_sem=rsend.at[k, j], recv_sem=rrecv.at[k, j],
            device_id=(blk - k, s), device_id_type=MESH,
        )

    for j in range(1, nu):
        terms(0, j, span).start()

    @pl.when(has_prev)
    def _():
        for j in range(nu):
            terms(1, j, 0).start()

    @pl.loop(0, chunks)
    def _(c):
        for a in range(2):
            for j in range(1, nu):
                across(a, j, c).wait_send()

            @pl.when(has_next)
            def _():
                for j in range(nu):
                    onward(a, j, c).wait_send()

    for j in range(1, nu):
        low_across(j).wait_send()

    @pl.when(has_next)
    def _():
        for j in range(nu):
            low_onward(j).wait_send()

    lrq[...] += lrv[mine, :]
    for j in range(1, nu):
        terms(0, j, span).wait_recv()
        lrq[...] += lrin[0, j]

    @pl.when(has_next)
    def _():
        for j in range(nu):
            terms(1, j, 0).wait_recv()
            lrq[...] += lrin[1, j]

    low_out[...] = lrq[...].astype(BF16)
    for j in range(1, nu):
        terms(0, j, span).wait_send()

    @pl.when(has_prev)
    def _():
        for j in range(nu):
            terms(1, j, 0).wait_send()


def attention(nb, nu, *operands):
    rows, width = operands[0].shape
    rank = operands[6].shape[0]
    span = nu * rows
    chunks = width // CHUNK
    dma = pltpu.SemaphoreType.DMA
    anywhere = pl.BlockSpec(memory_space=pl.ANY)
    here = pl.BlockSpec(memory_space=pltpu.VMEM)
    return pl.pallas_call(
        functools.partial(attention_kernel, nb, nu),
        out_shape=(
            jax.ShapeDtypeStruct((rows, width), BF16),
            jax.ShapeDtypeStruct((width // HEAD * 2 * rank, HEAD), BF16),
            jax.ShapeDtypeStruct((rows, 2 * rank), BF16),
        ),
        in_specs=[anywhere] * 9,
        out_specs=(here, here, here),
        scratch_shapes=[
            pltpu.VMEM((2 * span, width), BF16),
            pltpu.VMEM((2 * span, width), BF16),
            pltpu.VMEM((2 * span, 2 * rank), BF16),
            pltpu.VMEM((rows, width), BF16),
            pltpu.VMEM((rows, width), BF16),
            pltpu.VMEM((rows, width), BF16),
            pltpu.VMEM((width, rank), BF16),
            pltpu.VMEM((width, rank), BF16),
            pltpu.VMEM((2 * rank, width), BF16),
            pltpu.VMEM((rows, 2 * rank), F32),
            pltpu.VMEM((2 * span, 2 * rank), F32),
            pltpu.VMEM((2, nu, rows, 2 * rank), F32),
            dma((9,)),
            dma((2, nu, chunks)), dma((2, nu, chunks)),
            dma((2, nu, chunks)), dma((2, nu, chunks)),
            dma((nu,)), dma((nu,)), dma((nu,)), dma((nu,)),
            dma((2, nu)), dma((2, nu)),
        ],
        compiler_params=pltpu.CompilerParams(
            collective_id=0, has_side_effects=True, vmem_limit_bytes=65_000_000
        ),
    )(*operands)


def reduction_kernel(
    nb, nu,
    tokens, lowrank, gup,
    down_out, upq_out, upv_out,
    tok, terms, pair, part, slots, down, ups, flat,
    local_sem, psend, precv, ssend, srecv, bsend, brecv, csend, crecv,
):
    blk = lax.axis_index("blk")
    u = lax.axis_index("uly")
    core = lax.rem(blk, 2)
    chip = blk // 2
    other = chip * 2 + 1 - core
    half = nb // 2
    chips = half * nu
    rows, width = tokens.shape
    rank = upq_out.shape[0]
    region = pair.shape[2]
    piece = slots.shape[2]

    def peer_u(o):
        return lax.rem(u + o // half, nu)

    def peer_chip(o):
        return lax.rem(chip + lax.rem(o, half), half)

    def from_u(o):
        return lax.rem(u - o // half + nu, nu)

    def from_chip(o):
        return lax.rem(chip - lax.rem(o, half) + half, half)

    def at(c):
        return pl.ds(pl.multiple_of(c * piece, piece), piece)

    barrier = pltpu.get_barrier_semaphore()
    pl.semaphore_signal(barrier, inc=1, device_id=(other, u), device_id_type=MESH)

    @pl.loop(1, chips)
    def _(o):
        pl.semaphore_signal(
            barrier, inc=1, device_id=(peer_chip(o) * 2 + core, peer_u(o)), device_id_type=MESH
        )

    load = pltpu.make_async_copy(tokens, tok, local_sem.at[0])
    load.start()
    pl.semaphore_wait(barrier, chips)

    def swap(t, v):
        rows_at = pl.ds(pl.multiple_of((v * 2 + 1 - core) * region, region), region)
        return pltpu.make_async_remote_copy(
            src_ref=(terms if t == 0 else gup).at[rows_at], dst_ref=pair.at[t, v],
            send_sem=psend.at[t, v], recv_sem=precv.at[t, v],
            device_id=(other, u), device_id_type=MESH,
        )

    def scatter(t, o):
        return pltpu.make_async_remote_copy(
            src_ref=part.at[t, peer_u(o), at(peer_chip(o))], dst_ref=slots.at[t, o],
            send_sem=ssend.at[t, o], recv_sem=srecv.at[t, o],
            device_id=(peer_chip(o) * 2 + core, peer_u(o)), device_id_type=MESH,
        )

    def place(t, v, k, c):
        return down.at[v, k, at(c)] if t == 0 else ups.at[k, at(c)]

    def spread(t, o):
        mine = place(t, u, core, chip)
        return pltpu.make_async_remote_copy(
            src_ref=mine, dst_ref=mine, send_sem=bsend.at[t, o], recv_sem=brecv.at[t, o],
            device_id=(peer_chip(o) * 2 + core, peer_u(o)), device_id_type=MESH,
        )

    def landed(t, o):
        here = place(t, from_u(o), core, from_chip(o))
        return pltpu.make_async_remote_copy(
            src_ref=here, dst_ref=here, send_sem=bsend.at[t, o], recv_sem=brecv.at[t, o],
            device_id=(other, u), device_id_type=MESH,
        )

    def share(t, o):
        here = place(t, from_u(o), core, from_chip(o))
        return pltpu.make_async_remote_copy(
            src_ref=here, dst_ref=here, send_sem=csend.at[t, o], recv_sem=crecv.at[t, o],
            device_id=(other, u), device_id_type=MESH,
        )

    def shared(t, o):
        here = place(t, from_u(o), 1 - core, from_chip(o))
        return pltpu.make_async_remote_copy(
            src_ref=here, dst_ref=here, send_sem=csend.at[t, o], recv_sem=crecv.at[t, o],
            device_id=(other, u), device_id_type=MESH,
        )

    if part.shape[2] > region:
        part[...] = jnp.zeros_like(part)
    for v in range(nu):
        swap(1, v).start()

    load.wait()
    step = min(CHUNK, width)

    @pl.loop(0, width // step)
    def _(c):
        cols = pl.ds(pl.multiple_of(c * step, step), step)
        terms[cols, :] = inner(tok[:, cols], lowrank[...]).astype(BF16)

    def pair_sum(t):
        for v in range(nu):
            rows_at = pl.ds(pl.multiple_of((v * 2 + core) * region, region), region)
            own = (terms if t == 0 else gup)[rows_at, :]
            swap(t, v).wait_recv()
            part[t, v, pl.ds(0, region), :] = (
                own.astype(F32) + pair[t, v].astype(F32)
            ).astype(BF16)

    for v in range(nu):
        swap(0, v).start()
    for t in (1, 0):
        pair_sum(t)

        @pl.loop(1, chips)
        def _(o):
            scatter(t, o).start()

    counts = (chips, half)
    for t in (1, 0):

        def add(o, total):
            scatter(t, o).wait_recv()
            return total + slots[t, o].astype(F32)

        total = lax.fori_loop(1, chips, add, part[t, u, at(chip), :].astype(F32))
        if t == 0:
            down[u, core, at(chip), :] = total.astype(BF16)
        else:
            ups[core, at(chip), :] = total.astype(BF16)

        @pl.loop(1, counts[t])
        def _(o):
            spread(t, o).start()

        share(t, 0).start()

    for t in (1, 0):

        @pl.loop(1, counts[t])
        def _(o):
            landed(t, o).wait_recv()
            share(t, o).start()

    for t in (1, 0):

        @pl.loop(0, counts[t])
        def _(o):
            shared(t, o).wait_recv()

        if t == 1:
            for k in range(2):
                flat[pl.ds(k * region, region), :] = ups[k, pl.ds(0, region), :]
            for h in range(2 * region // (2 * rank)):
                cols = pl.ds(h * HEAD, HEAD)
                upq_out[:, cols] = flat[pl.ds(h * 2 * rank, rank), :]
                upv_out[:, cols] = flat[pl.ds(h * 2 * rank + rank, rank), :]
        else:
            for v in range(nu):
                for k in range(2):
                    down_out[pl.ds((v * 2 + k) * region, region), :] = down[
                        v, k, pl.ds(0, region), :
                    ]

    for t in (1, 0):
        for v in range(nu):
            swap(t, v).wait_send()

        @pl.loop(1, chips)
        def _(o):
            scatter(t, o).wait_send()

        @pl.loop(1, counts[t])
        def _(o):
            spread(t, o).wait_send()

        @pl.loop(0, counts[t])
        def _(o):
            share(t, o).wait_send()


def reduction(nb, nu, tokens, lowrank, gup):
    rows, width = tokens.shape
    rank = lowrank.shape[1] // 2
    half = nb // 2
    chips = half * nu
    region = width // (2 * nu)
    piece = -(-region // (16 * half)) * 16
    held = half * piece
    dma = pltpu.SemaphoreType.DMA
    here = pl.BlockSpec(memory_space=pltpu.VMEM)
    lanes = lowrank.shape[1]
    return pl.pallas_call(
        functools.partial(reduction_kernel, nb, nu),
        out_shape=(
            jax.ShapeDtypeStruct((width, lanes), BF16),
            jax.ShapeDtypeStruct((rank, width // nu), BF16),
            jax.ShapeDtypeStruct((rank, width // nu), BF16),
        ),
        in_specs=[pl.BlockSpec(memory_space=pl.ANY), here, here],
        out_specs=(here, here, here),
        scratch_shapes=[
            pltpu.VMEM((rows, width), BF16),
            pltpu.VMEM((width, lanes), BF16),
            pltpu.VMEM((2, nu, region, lanes), BF16),
            pltpu.VMEM((2, nu, held, lanes), BF16),
            pltpu.VMEM((2, chips, piece, lanes), BF16),
            pltpu.VMEM((nu, 2, held, lanes), BF16),
            pltpu.VMEM((2, held, lanes), BF16),
            pltpu.VMEM((2 * region, lanes), BF16),
            dma((1,)),
            dma((2, nu)), dma((2, nu)),
            dma((2, chips)), dma((2, chips)),
            dma((2, chips)), dma((2, chips)),
            dma((2, chips)), dma((2, chips)),
        ],
        compiler_params=pltpu.CompilerParams(collective_id=1, has_side_effects=True),
    )(tokens, lowrank, gup)


def per_device(nb, nu, tokens, query_base, key_base, value_base, out_grad, down_q, up_q, down_v, up_v):
    rank = down_q.shape[1]
    attended, gup, lowrank = attention(
        nb, nu, tokens, query_base, key_base, value_base, out_grad, down_q, up_q, down_v, up_v
    )
    down_total, grad_up_q, grad_up_v = reduction(nb, nu, tokens, lowrank, gup)
    return attended, down_total[:, :rank], grad_up_q, down_total[:, rank:], grad_up_v


def solution(mesh):
    split = P(("blk", "uly"), None)
    return jax.shard_map(
        functools.partial(per_device, mesh.shape["blk"], mesh.shape["uly"]),
        mesh=mesh,
        in_specs=(split,) * 5 + (P(),) * 4,
        out_specs=(split, P(), P(None, "uly"), P(), P(None, "uly")),
        check_vma=False,
    )
```

```python
import functools

import jax
import jax.numpy as jnp
from jax import lax
from jax.experimental import pallas as pl
from jax.experimental.pallas import tpu as pltpu
from jax.sharding import PartitionSpec as P

HEAD = 128
CHUNK = 512
MESH = pl.DeviceIdType.MESH
F32 = jnp.float32
BF16 = jnp.bfloat16


def inner(left, right):
    return lax.dot_general(left, right, (((0,), (0,)), ((), ())), preferred_element_type=F32)


def outer(left, right):
    return lax.dot_general(left, right, (((1,), (1,)), ((), ())), preferred_element_type=F32)


def dot(left, right):
    return jnp.dot(left, right, preferred_element_type=F32)


def attention_kernel(
    nb, nu,
    tokens, query_base, key_base, value_base, out_grad, down_q, up_q, down_v, up_v,
    att_ref, gup_ref, low_out,
    kbuf, vbuf, lbuf, tok, qs, gs, downs, ups, lrq, lrv, lrin,
    local_sem, xsend, xrecv, fsend, frecv, lsend, lrecv, msend, mrecv, rsend, rrecv,
):
    blk = lax.axis_index("blk")
    u = lax.axis_index("uly")
    rows, width = tokens.shape
    rank = up_q.shape[0]
    span = nu * rows
    chunks = width // CHUNK
    has_prev = blk > 0
    has_next = blk < nb - 1
    mine = pl.ds(pl.multiple_of(span + u * rows, rows), rows)

    def peer(j):
        return lax.rem(u + j, nu)

    def source(j):
        return lax.rem(u - j + nu, nu)

    def cols(c):
        return pl.ds(pl.multiple_of(c * CHUNK, CHUNK), CHUNK)

    barrier = pltpu.get_barrier_semaphore()
    for j in range(1, nu):
        pl.semaphore_signal(barrier, inc=1, device_id=(blk, peer(j)), device_id_type=MESH)

    @pl.when(has_prev)
    def _():
        for j in range(nu):
            pl.semaphore_signal(barrier, inc=1, device_id=(blk - 1, peer(j)), device_id_type=MESH)

    @pl.when(has_next)
    def _():
        for j in range(nu):
            pl.semaphore_signal(barrier, inc=1, device_id=(blk + 1, peer(j)), device_id_type=MESH)

    local = [
        pltpu.make_async_copy(src, dst, local_sem.at[i])
        for i, (src, dst) in enumerate(
            (
                (tokens, tok), (down_q, downs.at[pl.ds(0, rank)]), (down_v, downs.at[pl.ds(rank, rank)]),
                (up_q, ups.at[pl.ds(0, rank)]), (up_v, ups.at[pl.ds(rank, rank)]),
                (value_base, vbuf.at[mine]), (key_base, kbuf.at[mine]),
                (query_base, qs), (out_grad, gs),
            )
        )
    ]
    for copy in local:
        copy.start()

    edge = jnp.logical_or(blk == 0, blk == nb - 1)

    @pl.when(edge)
    def _():
        pl.semaphore_wait(barrier, 2 * nu - 1)

    @pl.when(jnp.logical_not(edge))
    def _():
        pl.semaphore_wait(barrier, 3 * nu - 1)

    bufs = (kbuf, vbuf)

    def across(a, j, c):
        src = key_base.at[:, cols(c)] if a == 0 else vbuf.at[mine, cols(c)]
        return pltpu.make_async_remote_copy(
            src_ref=src, dst_ref=bufs[a].at[mine, cols(c)],
            send_sem=xsend.at[a, j, c], recv_sem=xrecv.at[a, j, c],
            device_id=(blk, peer(j)), device_id_type=MESH,
        )

    def crossed(a, j, c):
        here = bufs[a].at[pl.ds(pl.multiple_of(span + source(j) * rows, rows), rows), cols(c)]
        return pltpu.make_async_remote_copy(
            src_ref=here, dst_ref=here,
            send_sem=xsend.at[a, j, c], recv_sem=xrecv.at[a, j, c],
            device_id=(blk, peer(j)), device_id_type=MESH,
        )

    def onward(a, j, c):
        s = source(j)
        if a == 0 and j == 0:
            src = key_base.at[:, cols(c)]
        else:
            src = bufs[a].at[pl.ds(pl.multiple_of(span + s * rows, rows), rows), cols(c)]
        return pltpu.make_async_remote_copy(
            src_ref=src, dst_ref=bufs[a].at[pl.ds(pl.multiple_of(s * rows, rows), rows), cols(c)],
            send_sem=fsend.at[a, j, c], recv_sem=frecv.at[a, j, c],
            device_id=(blk + 1, u), device_id_type=MESH,
        )

    def arrived(a, j, c):
        here = bufs[a].at[pl.ds(pl.multiple_of(source(j) * rows, rows), rows), cols(c)]
        return pltpu.make_async_remote_copy(
            src_ref=here, dst_ref=here,
            send_sem=fsend.at[a, j, c], recv_sem=frecv.at[a, j, c],
            device_id=(blk, peer(1)), device_id_type=MESH,
        )

    def low_across(j):
        return pltpu.make_async_remote_copy(
            src_ref=lbuf.at[mine], dst_ref=lbuf.at[mine],
            send_sem=lsend.at[j], recv_sem=lrecv.at[j],
            device_id=(blk, peer(j)), device_id_type=MESH,
        )

    def low_crossed(j):
        here = lbuf.at[pl.ds(pl.multiple_of(span + source(j) * rows, rows), rows)]
        return pltpu.make_async_remote_copy(
            src_ref=here, dst_ref=here, send_sem=lsend.at[j], recv_sem=lrecv.at[j],
            device_id=(blk, peer(j)), device_id_type=MESH,
        )

    def low_onward(j):
        s = source(j)
        return pltpu.make_async_remote_copy(
            src_ref=lbuf.at[pl.ds(pl.multiple_of(span + s * rows, rows), rows)],
            dst_ref=lbuf.at[pl.ds(pl.multiple_of(s * rows, rows), rows)],
            send_sem=msend.at[j], recv_sem=mrecv.at[j],
            device_id=(blk + 1, u), device_id_type=MESH,
        )

    def low_arrived(j):
        here = lbuf.at[pl.ds(pl.multiple_of(source(j) * rows, rows), rows)]
        return pltpu.make_async_remote_copy(
            src_ref=here, dst_ref=here, send_sem=msend.at[j], recv_sem=mrecv.at[j],
            device_id=(blk, peer(1)), device_id_type=MESH,
        )

    early = min(3, chunks)
    for c in range(early):
        for j in range(1, nu):
            across(0, j, c).start()

        @pl.when(has_next)
        def _():
            onward(0, 0, c).start()

    lane = lax.broadcasted_iota(jnp.int32, (rows, 2 * rank), 1)
    for i in range(3):
        local[i].wait()
    low = outer(tok[...], downs[...])
    low_qm = jnp.where(lane < rank, low, 0.0).astype(BF16)
    low_vm = jnp.where(lane >= rank, low, 0.0).astype(BF16)
    lbuf[mine, :] = low_vm
    for i in range(3, 6):
        local[i].wait()

    @pl.loop(0, chunks)
    def _(c):
        part = dot(low_vm, ups[:, cols(c)])
        vbuf[mine, cols(c)] = (vbuf[mine, cols(c)].astype(F32) + part).astype(BF16)

    for j in range(1, nu):
        low_across(j).start()

    @pl.when(has_next)
    def _():
        low_onward(0).start()

    @pl.loop(0, chunks)
    def _(c):
        @pl.when(c >= early)
        def _():
            for j in range(1, nu):
                across(0, j, c).start()

            @pl.when(has_next)
            def _():
                onward(0, 0, c).start()

        for j in range(1, nu):
            across(1, j, c).start()

        @pl.when(has_next)
        def _():
            onward(1, 0, c).start()

    lrq[...] = jnp.zeros_like(lrq)
    lrv[...] = jnp.zeros_like(lrv)

    @pl.when(jnp.logical_not(has_prev))
    def _():
        kbuf[pl.ds(0, span), :] = jnp.zeros((span, width), BF16)
        vbuf[pl.ds(0, span), :] = jnp.zeros((span, width), BF16)
        lbuf[pl.ds(0, span), :] = jnp.zeros((span, 2 * rank), BF16)

    for i in range(6, 9):
        local[i].wait()

    scale = HEAD ** (-0.5)
    key_at = lax.broadcasted_iota(jnp.int32, (rows, 2 * span), 1)
    usable = jnp.logical_or(key_at >= span, has_prev)

    def head(h):
        at = pl.ds(pl.multiple_of(h * HEAD, HEAD), HEAD)
        up = ups[:, at]
        keys = kbuf[:, at]
        values = vbuf[:, at]
        grad = gs[:, at]
        query = (qs[:, at].astype(F32) + dot(low_qm, up)).astype(BF16)
        scores = jnp.where(usable, outer(query, keys) * scale, -jnp.inf)
        weights = jnp.exp(scores - jnp.max(scores, axis=1, keepdims=True))
        total = jnp.sum(weights, axis=1, keepdims=True)
        probs = (weights * (1.0 / total)).astype(BF16)
        attended = dot(probs, values).astype(BF16)
        att_ref[:, at] = attended
        delta = jnp.sum(grad.astype(F32) * attended.astype(F32), axis=1, keepdims=True)
        score_grad = (probs.astype(F32) * (outer(grad, values) - delta)).astype(BF16)
        query_grad = (dot(score_grad, keys) * scale).astype(BF16)
        seen = dot(probs, lbuf[...]).astype(BF16)
        here = pl.ds(pl.multiple_of(h * 2 * rank, 2 * rank), 2 * rank)
        gup_ref[here, :] = (inner(low_qm, query_grad) + inner(seen, grad)).astype(BF16)
        lrq[...] += jnp.where(lane < rank, outer(query_grad, up), 0.0)
        lifted = jnp.where(lane >= rank, outer(grad, up), 0.0).astype(BF16)
        lrv[...] += inner(probs, lifted)

    heads = CHUNK // HEAD

    @pl.loop(0, chunks + 1)
    def _(c):
        @pl.when(c == 0)
        def _():
            for j in range(1, nu):
                low_crossed(j).wait_recv()

                @pl.when(has_next)
                def _():
                    low_onward(j).start()

            @pl.when(has_prev)
            def _():
                for j in range(nu):
                    low_arrived(j).wait_recv()

        @pl.when(c < chunks)
        def _():
            for a in range(2):
                for j in range(1, nu):
                    crossed(a, j, c).wait_recv()

                    @pl.when(has_next)
                    def _():
                        onward(a, j, c).start()

        @pl.when(c > 0)
        def _():
            @pl.when(has_prev)
            def _():
                for a in range(2):
                    for j in range(nu):
                        arrived(a, j, c - 1).wait_recv()

            @pl.loop(0, heads)
            def _(i):
                head((c - 1) * heads + i)

    def terms(k, j, base):
        s = peer(j)
        return pltpu.make_async_remote_copy(
            src_ref=lrv.at[pl.ds(pl.multiple_of(base + s * rows, rows), rows)],
            dst_ref=lrin.at[k, j],
            send_sem=rsend.at[k, j], recv_sem=rrecv.at[k, j],
            device_id=(blk - k, s), device_id_type=MESH,
        )

    for j in range(1, nu):
        terms(0, j, span).start()

    @pl.when(has_prev)
    def _():
        for j in range(nu):
            terms(1, j, 0).start()

    @pl.loop(0, chunks)
    def _(c):
        for a in range(2):
            for j in range(1, nu):
                across(a, j, c).wait_send()

            @pl.when(has_next)
            def _():
                for j in range(nu):
                    onward(a, j, c).wait_send()

    for j in range(1, nu):
        low_across(j).wait_send()

    @pl.when(has_next)
    def _():
        for j in range(nu):
            low_onward(j).wait_send()

    lrq[...] += lrv[mine, :]
    for j in range(1, nu):
        terms(0, j, span).wait_recv()
        lrq[...] += lrin[0, j]

    @pl.when(has_next)
    def _():
        for j in range(nu):
            terms(1, j, 0).wait_recv()
            lrq[...] += lrin[1, j]

    low_out[...] = lrq[...].astype(BF16)
    for j in range(1, nu):
        terms(0, j, span).wait_send()

    @pl.when(has_prev)
    def _():
        for j in range(nu):
            terms(1, j, 0).wait_send()


def attention(nb, nu, *operands):
    rows, width = operands[0].shape
    rank = operands[6].shape[0]
    span = nu * rows
    chunks = width // CHUNK
    dma = pltpu.SemaphoreType.DMA
    anywhere = pl.BlockSpec(memory_space=pl.ANY)
    here = pl.BlockSpec(memory_space=pltpu.VMEM)
    return pl.pallas_call(
        functools.partial(attention_kernel, nb, nu),
        out_shape=(
            jax.ShapeDtypeStruct((rows, width), BF16),
            jax.ShapeDtypeStruct((width // HEAD * 2 * rank, HEAD), BF16),
            jax.ShapeDtypeStruct((rows, 2 * rank), BF16),
        ),
        in_specs=[anywhere] * 9,
        out_specs=(here, here, here),
        scratch_shapes=[
            pltpu.VMEM((2 * span, width), BF16),
            pltpu.VMEM((2 * span, width), BF16),
            pltpu.VMEM((2 * span, 2 * rank), BF16),
            pltpu.VMEM((rows, width), BF16),
            pltpu.VMEM((rows, width), BF16),
            pltpu.VMEM((rows, width), BF16),
            pltpu.VMEM((2 * rank, width), BF16),
            pltpu.VMEM((2 * rank, width), BF16),
            pltpu.VMEM((rows, 2 * rank), F32),
            pltpu.VMEM((2 * span, 2 * rank), F32),
            pltpu.VMEM((2, nu, rows, 2 * rank), F32),
            dma((9,)),
            dma((2, nu, chunks)), dma((2, nu, chunks)),
            dma((2, nu, chunks)), dma((2, nu, chunks)),
            dma((nu,)), dma((nu,)), dma((nu,)), dma((nu,)),
            dma((2, nu)), dma((2, nu)),
        ],
        compiler_params=pltpu.CompilerParams(
            collective_id=0, has_side_effects=True, vmem_limit_bytes=65_000_000
        ),
    )(*operands)


def reduction_kernel(
    nb, nu,
    tokens, lowrank, gup,
    downq_out, downv_out, upq_out, upv_out,
    tok, terms, pair, part, plane_in, line, line_in, down, ups, flat,
    local_sem, psend, precv, asend, arecv, bsend, brecv, csend, crecv, dsend, drecv, esend, erecv,
):
    blk = lax.axis_index("blk")
    u = lax.axis_index("uly")
    core = lax.rem(blk, 2)
    chip = blk // 2
    other = chip * 2 + 1 - core
    half = nb // 2
    inners = plane_in.shape[1] // nu
    outers = half // inners
    y = lax.rem(chip, inners)
    z = chip // inners
    group = nu * inners
    rows, width = tokens.shape
    rank = upq_out.shape[0]
    region = pair.shape[2]
    sub = plane_in.shape[2]
    piece = line_in.shape[2]

    def split(o, sign):
        pu = lax.rem(u + sign * (o // inners) + nu, nu)
        py = lax.rem(y + sign * lax.rem(o, inners) + inners, inners)
        return pu, py

    def plane_dev(o):
        pu, py = split(o, 1)
        return ((z * inners + py) * 2 + core, pu)

    def peer_z(o):
        return lax.rem(z + o, outers)

    def from_z(o):
        return lax.rem(z - o + outers, outers)

    def line_dev(o):
        return ((peer_z(o) * inners + y) * 2 + core, u)

    def subs(p):
        return pl.ds(pl.multiple_of(p * sub, sub), sub)

    barrier = pltpu.get_barrier_semaphore()
    pl.semaphore_signal(barrier, inc=1, device_id=(other, u), device_id_type=MESH)
    for o in range(1, group):
        pl.semaphore_signal(barrier, inc=1, device_id=plane_dev(o), device_id_type=MESH)
    for o in range(1, outers):
        pl.semaphore_signal(barrier, inc=1, device_id=line_dev(o), device_id_type=MESH)

    load = pltpu.make_async_copy(tokens, tok, local_sem.at[0])
    load.start()
    pl.semaphore_wait(barrier, group + outers - 1)

    def remote(src, dst, send, recv, device):
        return pltpu.make_async_remote_copy(
            src_ref=src, dst_ref=dst, send_sem=send, recv_sem=recv,
            device_id=device, device_id_type=MESH,
        )

    def swap(t, v):
        rows_at = pl.ds(pl.multiple_of((v * 2 + 1 - core) * region, region), region)
        return remote(
            (terms if t == 0 else gup).at[rows_at], pair.at[t, v],
            psend.at[t, v], precv.at[t, v], (other, u),
        )

    def scatter(t, o):
        pu, py = split(o, 1)
        return remote(
            part.at[t, pu, subs(py)], plane_in.at[t, o],
            asend.at[t, o], arecv.at[t, o], plane_dev(o),
        )

    def pass_on(t, o):
        at = pl.ds(pl.multiple_of(peer_z(o) * piece, piece), piece)
        return remote(
            line.at[t, at], line_in.at[t, o], bsend.at[t, o], brecv.at[t, o], line_dev(o)
        )

    def whole(t, v, k, p):
        return down.at[v, k, subs(p)] if t == 0 else ups.at[k, subs(p)]

    def piece_at(p, q):
        return pl.ds(pl.multiple_of(p * sub + q * piece, piece), piece)

    def small(t, q):
        return down.at[u, core, piece_at(y, q)] if t == 0 else ups.at[core, piece_at(y, q)]

    def along(t, o):
        return remote(small(t, z), small(t, z), csend.at[t, o], crecv.at[t, o], line_dev(o))

    def came(t, o):
        here = small(t, from_z(o))
        return remote(here, here, csend.at[t, o], crecv.at[t, o], line_dev(o))

    def spread(t, o):
        here = whole(t, u, core, y)
        return remote(here, here, dsend.at[t, o], drecv.at[t, o], plane_dev(o))

    def landed(t, o):
        pu, py = split(o, -1)
        here = whole(t, pu, core, py)
        return remote(here, here, dsend.at[t, o], drecv.at[t, o], (other, u))

    def share(t, o):
        pu, py = split(o, -1)
        here = whole(t, pu, core, py)
        return remote(here, here, esend.at[t, o], erecv.at[t, o], (other, u))

    def shared(t, o):
        pu, py = split(o, -1)
        here = whole(t, pu, 1 - core, py)
        return remote(here, here, esend.at[t, o], erecv.at[t, o], (other, u))

    if part.shape[2] > region:
        part[...] = jnp.zeros_like(part)
    for v in range(nu):
        swap(1, v).start()

    load.wait()
    lows = lowrank[...]

    @pl.loop(0, width // HEAD)
    def _(h):
        cols = pl.ds(pl.multiple_of(h * HEAD, HEAD), HEAD)
        here = pl.ds(pl.multiple_of(h * 2 * rank, 2 * rank), 2 * rank)
        terms[here, :] = inner(lows, tok[:, cols]).astype(BF16)

    for v in range(nu):
        swap(0, v).start()

    for t in (1, 0):
        for v in range(nu):
            rows_at = pl.ds(pl.multiple_of((v * 2 + core) * region, region), region)
            own = (terms if t == 0 else gup)[rows_at, :]
            swap(t, v).wait_recv()
            part[t, v, pl.ds(0, region), :] = (
                own.astype(F32) + pair[t, v].astype(F32)
            ).astype(BF16)
        for o in range(1, group):
            scatter(t, o).start()

    for t in (1, 0):
        total = part[t, u, subs(y), :].astype(F32)
        for o in range(1, group):
            scatter(t, o).wait_recv()
            total = total + plane_in[t, o].astype(F32)
        line[t, :, :] = total.astype(BF16)
        for o in range(1, outers):
            pass_on(t, o).start()

    for t in (1, 0):
        total = line[t, pl.ds(pl.multiple_of(z * piece, piece), piece), :].astype(F32)
        for o in range(1, outers):
            pass_on(t, o).wait_recv()
            total = total + line_in[t, o].astype(F32)
        small(t, z)[...] = total.astype(BF16)
        for o in range(1, outers):
            along(t, o).start()

    counts = (group, inners)
    for t in (1, 0):
        for o in range(1, outers):
            came(t, o).wait_recv()
        for o in range(1, counts[t]):
            spread(t, o).start()
        share(t, 0).start()

    for t in (1, 0):
        for o in range(1, counts[t]):
            landed(t, o).wait_recv()
            share(t, o).start()

    for t in (1, 0):
        for o in range(counts[t]):
            shared(t, o).wait_recv()
        places = [(v, k) for v in range(nu if t == 0 else 1) for k in range(2)]
        for n, (v, k) in enumerate(places):
            flat[pl.ds(n * region, region), :] = (
                down[v, k, pl.ds(0, region), :] if t == 0 else ups[k, pl.ds(0, region), :]
            )
        outs = (downq_out, downv_out) if t == 0 else (upq_out, upv_out)
        for h in range(len(places) * region // (2 * rank)):
            cols = pl.ds(h * HEAD, HEAD)
            outs[0][:, cols] = flat[pl.ds(h * 2 * rank, rank), :]
            outs[1][:, cols] = flat[pl.ds(h * 2 * rank + rank, rank), :]

    for t in (1, 0):
        for v in range(nu):
            swap(t, v).wait_send()
        for o in range(1, group):
            scatter(t, o).wait_send()
        for o in range(1, outers):
            pass_on(t, o).wait_send()
            along(t, o).wait_send()
        for o in range(1, counts[t]):
            spread(t, o).wait_send()
        for o in range(counts[t]):
            share(t, o).wait_send()


def reduction(nb, nu, tokens, lowrank, gup):
    rows, width = tokens.shape
    rank = lowrank.shape[1] // 2
    half = nb // 2
    inners = 2 if half % 2 == 0 else 1
    outers = half // inners
    group = nu * inners
    region = width // (2 * nu)
    piece = -(-region // (16 * half)) * 16
    sub = outers * piece
    held = half * piece
    dma = pltpu.SemaphoreType.DMA
    here = pl.BlockSpec(memory_space=pltpu.VMEM)
    lanes = lowrank.shape[1]
    return pl.pallas_call(
        functools.partial(reduction_kernel, nb, nu),
        out_shape=(
            jax.ShapeDtypeStruct((rank, width), BF16),
            jax.ShapeDtypeStruct((rank, width), BF16),
            jax.ShapeDtypeStruct((rank, width // nu), BF16),
            jax.ShapeDtypeStruct((rank, width // nu), BF16),
        ),
        in_specs=[pl.BlockSpec(memory_space=pl.ANY), here, here],
        out_specs=(here, here, here, here),
        scratch_shapes=[
            pltpu.VMEM((rows, width), BF16),
            pltpu.VMEM((width, lanes), BF16),
            pltpu.VMEM((2, nu, region, lanes), BF16),
            pltpu.VMEM((2, nu, held, lanes), BF16),
            pltpu.VMEM((2, group, sub, lanes), BF16),
            pltpu.VMEM((2, sub, lanes), BF16),
            pltpu.VMEM((2, outers, piece, lanes), BF16),
            pltpu.VMEM((nu, 2, held, lanes), BF16),
            pltpu.VMEM((2, held, lanes), BF16),
            pltpu.VMEM((2 * nu * region, lanes), BF16),
            dma((1,)),
            dma((2, nu)), dma((2, nu)),
            dma((2, group)), dma((2, group)),
            dma((2, outers)), dma((2, outers)),
            dma((2, outers)), dma((2, outers)),
            dma((2, group)), dma((2, group)),
            dma((2, group)), dma((2, group)),
        ],
        compiler_params=pltpu.CompilerParams(collective_id=1, has_side_effects=True),
    )(tokens, lowrank, gup)


def per_device(nb, nu, tokens, query_base, key_base, value_base, out_grad, down_q, up_q, down_v, up_v):
    attended, gup, lowrank = attention(
        nb, nu, tokens, query_base, key_base, value_base, out_grad, down_q.T, up_q, down_v.T, up_v
    )
    grad_down_q, grad_down_v, grad_up_q, grad_up_v = reduction(nb, nu, tokens, lowrank, gup)
    return attended, grad_down_q.T, grad_up_q, grad_down_v.T, grad_up_v


def solution(mesh):
    split = P(("blk", "uly"), None)
    return jax.shard_map(
        functools.partial(per_device, mesh.shape["blk"], mesh.shape["uly"]),
        mesh=mesh,
        in_specs=(split,) * 5 + (P(),) * 4,
        out_specs=(split, P(), P(None, "uly"), P(), P(None, "uly")),
        check_vma=False,
    )
```

```python
import functools

import jax
import jax.numpy as jnp
from jax import lax
from jax.experimental import pallas as pl
from jax.experimental.pallas import tpu as pltpu
from jax.sharding import PartitionSpec as P

HEAD = 128
CHUNK = 512
MESH = pl.DeviceIdType.MESH
F32 = jnp.float32
BF16 = jnp.bfloat16


def inner(left, right):
    return lax.dot_general(left, right, (((0,), (0,)), ((), ())), preferred_element_type=F32)


def outer(left, right):
    return lax.dot_general(left, right, (((1,), (1,)), ((), ())), preferred_element_type=F32)


def dot(left, right):
    return jnp.dot(left, right, preferred_element_type=F32)


def attention_kernel(
    nb, nu,
    tokens, query_base, key_base, value_base, out_grad, down_q, up_q, down_v, up_v,
    att_ref, gup_ref, low_out,
    kbuf, vbuf, lbuf, tok, qs, gs, downs, ups, lrq, lrv, lrin,
    local_sem, xsend, xrecv, fsend, frecv, lsend, lrecv, msend, mrecv, rsend, rrecv,
):
    blk = lax.axis_index("blk")
    u = lax.axis_index("uly")
    rows, width = tokens.shape
    rank = up_q.shape[0]
    span = nu * rows
    chunks = width // CHUNK
    has_prev = blk > 0
    has_next = blk < nb - 1
    mine = pl.ds(pl.multiple_of(span + u * rows, rows), rows)

    def peer(j):
        return lax.rem(u + j, nu)

    def source(j):
        return lax.rem(u - j + nu, nu)

    def cols(c):
        return pl.ds(pl.multiple_of(c * CHUNK, CHUNK), CHUNK)

    barrier = pltpu.get_barrier_semaphore()
    for j in range(1, nu):
        pl.semaphore_signal(barrier, inc=1, device_id=(blk, peer(j)), device_id_type=MESH)

    @pl.when(has_prev)
    def _():
        for j in range(nu):
            pl.semaphore_signal(barrier, inc=1, device_id=(blk - 1, peer(j)), device_id_type=MESH)

    @pl.when(has_next)
    def _():
        for j in range(nu):
            pl.semaphore_signal(barrier, inc=1, device_id=(blk + 1, peer(j)), device_id_type=MESH)

    local = [
        pltpu.make_async_copy(src, dst, local_sem.at[i])
        for i, (src, dst) in enumerate(
            (
                (tokens, tok), (down_q, downs.at[pl.ds(0, rank)]), (down_v, downs.at[pl.ds(rank, rank)]),
                (up_q, ups.at[pl.ds(0, rank)]), (up_v, ups.at[pl.ds(rank, rank)]),
                (value_base, vbuf.at[mine]), (key_base, kbuf.at[mine]),
                (query_base, qs), (out_grad, gs),
            )
        )
    ]
    for copy in local:
        copy.start()

    edge = jnp.logical_or(blk == 0, blk == nb - 1)

    @pl.when(edge)
    def _():
        pl.semaphore_wait(barrier, 2 * nu - 1)

    @pl.when(jnp.logical_not(edge))
    def _():
        pl.semaphore_wait(barrier, 3 * nu - 1)

    bufs = (kbuf, vbuf)

    def across(a, j, c):
        src = key_base.at[:, cols(c)] if a == 0 else vbuf.at[mine, cols(c)]
        return pltpu.make_async_remote_copy(
            src_ref=src, dst_ref=bufs[a].at[mine, cols(c)],
            send_sem=xsend.at[a, j, c], recv_sem=xrecv.at[a, j, c],
            device_id=(blk, peer(j)), device_id_type=MESH,
        )

    def crossed(a, j, c):
        here = bufs[a].at[pl.ds(pl.multiple_of(span + source(j) * rows, rows), rows), cols(c)]
        return pltpu.make_async_remote_copy(
            src_ref=here, dst_ref=here,
            send_sem=xsend.at[a, j, c], recv_sem=xrecv.at[a, j, c],
            device_id=(blk, peer(j)), device_id_type=MESH,
        )

    def onward(a, j, c):
        s = source(j)
        if a == 0 and j == 0:
            src = key_base.at[:, cols(c)]
        else:
            src = bufs[a].at[pl.ds(pl.multiple_of(span + s * rows, rows), rows), cols(c)]
        return pltpu.make_async_remote_copy(
            src_ref=src, dst_ref=bufs[a].at[pl.ds(pl.multiple_of(s * rows, rows), rows), cols(c)],
            send_sem=fsend.at[a, j, c], recv_sem=frecv.at[a, j, c],
            device_id=(blk + 1, u), device_id_type=MESH,
        )

    def arrived(a, j, c):
        here = bufs[a].at[pl.ds(pl.multiple_of(source(j) * rows, rows), rows), cols(c)]
        return pltpu.make_async_remote_copy(
            src_ref=here, dst_ref=here,
            send_sem=fsend.at[a, j, c], recv_sem=frecv.at[a, j, c],
            device_id=(blk, peer(1)), device_id_type=MESH,
        )

    def low_across(j):
        return pltpu.make_async_remote_copy(
            src_ref=lbuf.at[mine], dst_ref=lbuf.at[mine],
            send_sem=lsend.at[j], recv_sem=lrecv.at[j],
            device_id=(blk, peer(j)), device_id_type=MESH,
        )

    def low_crossed(j):
        here = lbuf.at[pl.ds(pl.multiple_of(span + source(j) * rows, rows), rows)]
        return pltpu.make_async_remote_copy(
            src_ref=here, dst_ref=here, send_sem=lsend.at[j], recv_sem=lrecv.at[j],
            device_id=(blk, peer(j)), device_id_type=MESH,
        )

    def low_onward(j):
        s = source(j)
        return pltpu.make_async_remote_copy(
            src_ref=lbuf.at[pl.ds(pl.multiple_of(span + s * rows, rows), rows)],
            dst_ref=lbuf.at[pl.ds(pl.multiple_of(s * rows, rows), rows)],
            send_sem=msend.at[j], recv_sem=mrecv.at[j],
            device_id=(blk + 1, u), device_id_type=MESH,
        )

    def low_arrived(j):
        here = lbuf.at[pl.ds(pl.multiple_of(source(j) * rows, rows), rows)]
        return pltpu.make_async_remote_copy(
            src_ref=here, dst_ref=here, send_sem=msend.at[j], recv_sem=mrecv.at[j],
            device_id=(blk, peer(1)), device_id_type=MESH,
        )

    early = min(3, chunks)
    for c in range(early):
        for j in range(1, nu):
            across(0, j, c).start()

        @pl.when(has_next)
        def _():
            onward(0, 0, c).start()

    lane = lax.broadcasted_iota(jnp.int32, (rows, 2 * rank), 1)
    for i in range(3):
        local[i].wait()
    low = outer(tok[...], downs[...])
    low_qm = jnp.where(lane < rank, low, 0.0).astype(BF16)
    low_vm = jnp.where(lane >= rank, low, 0.0).astype(BF16)
    lbuf[mine, :] = low_vm
    for i in range(3, 6):
        local[i].wait()

    @pl.loop(0, chunks)
    def _(c):
        part = dot(low_vm, ups[:, cols(c)])
        vbuf[mine, cols(c)] = (vbuf[mine, cols(c)].astype(F32) + part).astype(BF16)

    for j in range(1, nu):
        low_across(j).start()

    @pl.when(has_next)
    def _():
        low_onward(0).start()

    @pl.loop(0, chunks)
    def _(c):
        @pl.when(c >= early)
        def _():
            for j in range(1, nu):
                across(0, j, c).start()

            @pl.when(has_next)
            def _():
                onward(0, 0, c).start()

        for j in range(1, nu):
            across(1, j, c).start()

        @pl.when(has_next)
        def _():
            onward(1, 0, c).start()

    lrq[...] = jnp.zeros_like(lrq)
    lrv[...] = jnp.zeros_like(lrv)

    @pl.when(jnp.logical_not(has_prev))
    def _():
        kbuf[pl.ds(0, span), :] = jnp.zeros((span, width), BF16)
        vbuf[pl.ds(0, span), :] = jnp.zeros((span, width), BF16)
        lbuf[pl.ds(0, span), :] = jnp.zeros((span, 2 * rank), BF16)

    for i in range(6, 9):
        local[i].wait()

    scale = HEAD ** (-0.5)
    key_at = lax.broadcasted_iota(jnp.int32, (rows, 2 * span), 1)
    usable = jnp.logical_or(key_at >= span, has_prev)

    def head(h):
        at = pl.ds(pl.multiple_of(h * HEAD, HEAD), HEAD)
        up = ups[:, at]
        keys = kbuf[:, at]
        values = vbuf[:, at]
        grad = gs[:, at]
        query = (qs[:, at].astype(F32) + dot(low_qm, up)).astype(BF16)
        scores = jnp.where(usable, outer(query, keys) * scale, -jnp.inf)
        weights = jnp.exp(scores - jnp.max(scores, axis=1, keepdims=True))
        total = jnp.sum(weights, axis=1, keepdims=True)
        probs = (weights * (1.0 / total)).astype(BF16)
        attended = dot(probs, values).astype(BF16)
        delta = jnp.sum(grad.astype(F32) * attended.astype(F32), axis=1, keepdims=True)
        score_grad = (probs.astype(F32) * (outer(grad, values) - delta)).astype(BF16)
        query_grad = (dot(score_grad, keys) * scale).astype(BF16)
        seen = dot(probs, lbuf[...]).astype(BF16)
        gup = (inner(low_qm, query_grad) + inner(seen, grad)).astype(BF16)
        lifted = jnp.where(lane >= rank, outer(grad, up), 0.0).astype(BF16)
        return attended, gup, outer(query_grad, up), inner(probs, lifted)

    together = 2 if span <= 2 * HEAD else 1

    def head_group(first):
        results = [head(first + i) for i in range(together)]
        for i, (attended, gup, _, _) in enumerate(results):
            h = first + i
            att_ref[:, pl.ds(pl.multiple_of(h * HEAD, HEAD), HEAD)] = attended
            gup_ref[pl.ds(pl.multiple_of(h * 2 * rank, 2 * rank), 2 * rank), :] = gup
        lrq[...] += jnp.where(lane < rank, sum(r[2] for r in results), 0.0)
        lrv[...] += sum(r[3] for r in results)

    heads = CHUNK // HEAD

    @pl.loop(0, chunks + 1)
    def _(c):
        @pl.when(c == 0)
        def _():
            for j in range(1, nu):
                low_crossed(j).wait_recv()

                @pl.when(has_next)
                def _():
                    low_onward(j).start()

            @pl.when(has_prev)
            def _():
                for j in range(nu):
                    low_arrived(j).wait_recv()

        @pl.when(c < chunks)
        def _():
            for a in range(2):
                for j in range(1, nu):
                    crossed(a, j, c).wait_recv()

                    @pl.when(has_next)
                    def _():
                        onward(a, j, c).start()

        @pl.when(c > 0)
        def _():
            @pl.when(has_prev)
            def _():
                for a in range(2):
                    for j in range(nu):
                        arrived(a, j, c - 1).wait_recv()

            @pl.loop(0, heads // together)
            def _(i):
                head_group((c - 1) * heads + i * together)

    def terms(k, j, base):
        s = peer(j)
        return pltpu.make_async_remote_copy(
            src_ref=lrv.at[pl.ds(pl.multiple_of(base + s * rows, rows), rows)],
            dst_ref=lrin.at[k, j],
            send_sem=rsend.at[k, j], recv_sem=rrecv.at[k, j],
            device_id=(blk - k, s), device_id_type=MESH,
        )

    for j in range(1, nu):
        terms(0, j, span).start()

    @pl.when(has_prev)
    def _():
        for j in range(nu):
            terms(1, j, 0).start()

    @pl.loop(0, chunks)
    def _(c):
        for a in range(2):
            for j in range(1, nu):
                across(a, j, c).wait_send()

            @pl.when(has_next)
            def _():
                for j in range(nu):
                    onward(a, j, c).wait_send()

    for j in range(1, nu):
        low_across(j).wait_send()

    @pl.when(has_next)
    def _():
        for j in range(nu):
            low_onward(j).wait_send()

    lrq[...] += lrv[mine, :]
    for j in range(1, nu):
        terms(0, j, span).wait_recv()
        lrq[...] += lrin[0, j]

    @pl.when(has_next)
    def _():
        for j in range(nu):
            terms(1, j, 0).wait_recv()
            lrq[...] += lrin[1, j]

    low_out[...] = lrq[...].astype(BF16)
    for j in range(1, nu):
        terms(0, j, span).wait_send()

    @pl.when(has_prev)
    def _():
        for j in range(nu):
            terms(1, j, 0).wait_send()


def attention(nb, nu, *operands):
    rows, width = operands[0].shape
    rank = operands[6].shape[0]
    span = nu * rows
    chunks = width // CHUNK
    dma = pltpu.SemaphoreType.DMA
    anywhere = pl.BlockSpec(memory_space=pl.ANY)
    here = pl.BlockSpec(memory_space=pltpu.VMEM)
    return pl.pallas_call(
        functools.partial(attention_kernel, nb, nu),
        out_shape=(
            jax.ShapeDtypeStruct((rows, width), BF16),
            jax.ShapeDtypeStruct((width // HEAD * 2 * rank, HEAD), BF16),
            jax.ShapeDtypeStruct((rows, 2 * rank), BF16),
        ),
        in_specs=[anywhere] * 9,
        out_specs=(here, here, here),
        scratch_shapes=[
            pltpu.VMEM((2 * span, width), BF16),
            pltpu.VMEM((2 * span, width), BF16),
            pltpu.VMEM((2 * span, 2 * rank), BF16),
            pltpu.VMEM((rows, width), BF16),
            pltpu.VMEM((rows, width), BF16),
            pltpu.VMEM((rows, width), BF16),
            pltpu.VMEM((2 * rank, width), BF16),
            pltpu.VMEM((2 * rank, width), BF16),
            pltpu.VMEM((rows, 2 * rank), F32),
            pltpu.VMEM((2 * span, 2 * rank), F32),
            pltpu.VMEM((2, nu, rows, 2 * rank), F32),
            dma((9,)),
            dma((2, nu, chunks)), dma((2, nu, chunks)),
            dma((2, nu, chunks)), dma((2, nu, chunks)),
            dma((nu,)), dma((nu,)), dma((nu,)), dma((nu,)),
            dma((2, nu)), dma((2, nu)),
        ],
        compiler_params=pltpu.CompilerParams(
            collective_id=0, has_side_effects=True, vmem_limit_bytes=65_000_000
        ),
    )(*operands)


def reduction_kernel(
    nb, nu,
    tokens, lowrank, gup,
    downq_out, downv_out, upq_out, upv_out,
    tok, terms, pair, part, plane_in, line, line_in, down, ups, flat,
    local_sem, psend, precv, asend, arecv, bsend, brecv, csend, crecv, dsend, drecv, esend, erecv,
):
    blk = lax.axis_index("blk")
    u = lax.axis_index("uly")
    core = lax.rem(blk, 2)
    chip = blk // 2
    other = chip * 2 + 1 - core
    half = nb // 2
    inners = plane_in.shape[1] // nu
    outers = half // inners
    y = lax.rem(chip, inners)
    z = chip // inners
    group = nu * inners
    rows, width = tokens.shape
    rank = upq_out.shape[0]
    region = pair.shape[2]
    sub = plane_in.shape[2]
    piece = line_in.shape[2]

    def split(o, sign):
        pu = lax.rem(u + sign * (o // inners) + nu, nu)
        py = lax.rem(y + sign * lax.rem(o, inners) + inners, inners)
        return pu, py

    def plane_dev(o):
        pu, py = split(o, 1)
        return ((z * inners + py) * 2 + core, pu)

    def peer_z(o):
        return lax.rem(z + o, outers)

    def from_z(o):
        return lax.rem(z - o + outers, outers)

    def line_dev(o):
        return ((peer_z(o) * inners + y) * 2 + core, u)

    def subs(p):
        return pl.ds(pl.multiple_of(p * sub, sub), sub)

    barrier = pltpu.get_barrier_semaphore()
    pl.semaphore_signal(barrier, inc=1, device_id=(other, u), device_id_type=MESH)
    for o in range(1, group):
        pl.semaphore_signal(barrier, inc=1, device_id=plane_dev(o), device_id_type=MESH)
    for o in range(1, outers):
        pl.semaphore_signal(barrier, inc=1, device_id=line_dev(o), device_id_type=MESH)

    load = pltpu.make_async_copy(tokens, tok, local_sem.at[0])
    load.start()
    pl.semaphore_wait(barrier, group + outers - 1)

    def remote(src, dst, send, recv, device):
        return pltpu.make_async_remote_copy(
            src_ref=src, dst_ref=dst, send_sem=send, recv_sem=recv,
            device_id=device, device_id_type=MESH,
        )

    def swap(t, v):
        rows_at = pl.ds(pl.multiple_of((v * 2 + 1 - core) * region, region), region)
        return remote(
            (terms if t == 0 else gup).at[rows_at], pair.at[t, v],
            psend.at[t, v], precv.at[t, v], (other, u),
        )

    def scatter(t, o):
        pu, py = split(o, 1)
        return remote(
            part.at[t, pu, subs(py)], plane_in.at[t, o],
            asend.at[t, o], arecv.at[t, o], plane_dev(o),
        )

    def pass_on(t, o):
        at = pl.ds(pl.multiple_of(peer_z(o) * piece, piece), piece)
        return remote(
            line.at[t, at], line_in.at[t, o], bsend.at[t, o], brecv.at[t, o], line_dev(o)
        )

    def whole(t, v, k, p):
        return down.at[v, k, subs(p)] if t == 0 else ups.at[k, subs(p)]

    def piece_at(p, q):
        return pl.ds(pl.multiple_of(p * sub + q * piece, piece), piece)

    def small(t, q):
        return down.at[u, core, piece_at(y, q)] if t == 0 else ups.at[core, piece_at(y, q)]

    def along(t, o):
        return remote(small(t, z), small(t, z), csend.at[t, o], crecv.at[t, o], line_dev(o))

    def came(t, o):
        here = small(t, from_z(o))
        return remote(here, here, csend.at[t, o], crecv.at[t, o], line_dev(o))

    def spread(t, o):
        here = whole(t, u, core, y)
        return remote(here, here, dsend.at[t, o], drecv.at[t, o], plane_dev(o))

    def landed(t, o):
        pu, py = split(o, -1)
        here = whole(t, pu, core, py)
        return remote(here, here, dsend.at[t, o], drecv.at[t, o], (other, u))

    def share(t, o):
        pu, py = split(o, -1)
        here = whole(t, pu, core, py)
        return remote(here, here, esend.at[t, o], erecv.at[t, o], (other, u))

    def shared(t, o):
        pu, py = split(o, -1)
        here = whole(t, pu, 1 - core, py)
        return remote(here, here, esend.at[t, o], erecv.at[t, o], (other, u))

    if part.shape[2] > region:
        part[...] = jnp.zeros_like(part)
    for v in range(nu):
        swap(1, v).start()

    load.wait()
    lows = lowrank[...]

    @pl.loop(0, width // HEAD)
    def _(h):
        cols = pl.ds(pl.multiple_of(h * HEAD, HEAD), HEAD)
        here = pl.ds(pl.multiple_of(h * 2 * rank, 2 * rank), 2 * rank)
        terms[here, :] = inner(lows, tok[:, cols]).astype(BF16)

    for v in range(nu):
        swap(0, v).start()

    for t in (1, 0):
        for v in range(nu):
            rows_at = pl.ds(pl.multiple_of((v * 2 + core) * region, region), region)
            own = (terms if t == 0 else gup)[rows_at, :]
            swap(t, v).wait_recv()
            part[t, v, pl.ds(0, region), :] = (
                own.astype(F32) + pair[t, v].astype(F32)
            ).astype(BF16)
        for o in range(1, group):
            scatter(t, o).start()

    for t in (1, 0):
        total = part[t, u, subs(y), :].astype(F32)
        for o in range(1, group):
            scatter(t, o).wait_recv()
            total = total + plane_in[t, o].astype(F32)
        line[t, :, :] = total.astype(BF16)
        for o in range(1, outers):
            pass_on(t, o).start()

    for t in (1, 0):
        total = line[t, pl.ds(pl.multiple_of(z * piece, piece), piece), :].astype(F32)
        for o in range(1, outers):
            pass_on(t, o).wait_recv()
            total = total + line_in[t, o].astype(F32)
        small(t, z)[...] = total.astype(BF16)
        for o in range(1, outers):
            along(t, o).start()

    counts = (group, inners)
    for t in (1, 0):
        for o in range(1, outers):
            came(t, o).wait_recv()
        for o in range(1, counts[t]):
            spread(t, o).start()
        share(t, 0).start()

    for t in (1, 0):
        for o in range(1, counts[t]):
            landed(t, o).wait_recv()
            share(t, o).start()

    for t in (1, 0):
        for o in range(counts[t]):
            shared(t, o).wait_recv()
        places = [(v, k) for v in range(nu if t == 0 else 1) for k in range(2)]
        for n, (v, k) in enumerate(places):
            flat[pl.ds(n * region, region), :] = (
                down[v, k, pl.ds(0, region), :] if t == 0 else ups[k, pl.ds(0, region), :]
            )
        outs = (downq_out, downv_out) if t == 0 else (upq_out, upv_out)
        for h in range(len(places) * region // (2 * rank)):
            cols = pl.ds(h * HEAD, HEAD)
            outs[0][:, cols] = flat[pl.ds(h * 2 * rank, rank), :]
            outs[1][:, cols] = flat[pl.ds(h * 2 * rank + rank, rank), :]

    for t in (1, 0):
        for v in range(nu):
            swap(t, v).wait_send()
        for o in range(1, group):
            scatter(t, o).wait_send()
        for o in range(1, outers):
            pass_on(t, o).wait_send()
            along(t, o).wait_send()
        for o in range(1, counts[t]):
            spread(t, o).wait_send()
        for o in range(counts[t]):
            share(t, o).wait_send()


def reduction(nb, nu, tokens, lowrank, gup):
    rows, width = tokens.shape
    rank = lowrank.shape[1] // 2
    half = nb // 2
    inners = 2 if half % 2 == 0 else 1
    outers = half // inners
    group = nu * inners
    region = width // (2 * nu)
    piece = -(-region // (16 * half)) * 16
    sub = outers * piece
    held = half * piece
    dma = pltpu.SemaphoreType.DMA
    here = pl.BlockSpec(memory_space=pltpu.VMEM)
    lanes = lowrank.shape[1]
    return pl.pallas_call(
        functools.partial(reduction_kernel, nb, nu),
        out_shape=(
            jax.ShapeDtypeStruct((rank, width), BF16),
            jax.ShapeDtypeStruct((rank, width), BF16),
            jax.ShapeDtypeStruct((rank, width // nu), BF16),
            jax.ShapeDtypeStruct((rank, width // nu), BF16),
        ),
        in_specs=[pl.BlockSpec(memory_space=pl.ANY), here, here],
        out_specs=(here, here, here, here),
        scratch_shapes=[
            pltpu.VMEM((rows, width), BF16),
            pltpu.VMEM((width, lanes), BF16),
            pltpu.VMEM((2, nu, region, lanes), BF16),
            pltpu.VMEM((2, nu, held, lanes), BF16),
            pltpu.VMEM((2, group, sub, lanes), BF16),
            pltpu.VMEM((2, sub, lanes), BF16),
            pltpu.VMEM((2, outers, piece, lanes), BF16),
            pltpu.VMEM((nu, 2, held, lanes), BF16),
            pltpu.VMEM((2, held, lanes), BF16),
            pltpu.VMEM((2 * nu * region, lanes), BF16),
            dma((1,)),
            dma((2, nu)), dma((2, nu)),
            dma((2, group)), dma((2, group)),
            dma((2, outers)), dma((2, outers)),
            dma((2, outers)), dma((2, outers)),
            dma((2, group)), dma((2, group)),
            dma((2, group)), dma((2, group)),
        ],
        compiler_params=pltpu.CompilerParams(collective_id=1, has_side_effects=True),
    )(tokens, lowrank, gup)


def per_device(nb, nu, tokens, query_base, key_base, value_base, out_grad, down_q, up_q, down_v, up_v):
    attended, gup, lowrank = attention(
        nb, nu, tokens, query_base, key_base, value_base, out_grad, down_q.T, up_q, down_v.T, up_v
    )
    grad_down_q, grad_down_v, grad_up_q, grad_up_v = reduction(nb, nu, tokens, lowrank, gup)
    return attended, grad_down_q.T, grad_up_q, grad_down_v.T, grad_up_v


def solution(mesh):
    split = P(("blk", "uly"), None)
    return jax.shard_map(
        functools.partial(per_device, mesh.shape["blk"], mesh.shape["uly"]),
        mesh=mesh,
        in_specs=(split,) * 5 + (P(),) * 4,
        out_specs=(split, P(), P(None, "uly"), P(), P(None, "uly")),
        check_vma=False,
    )
```
